32 devices in a mesh: dp: 8 (over z, x), tensor: 4 (over y, core).
Axes of the slice: x: 2, y: 2, z: 4, core: 2. Of those that a mesh axis runs over, the one named last changes fastest.
Arguments:
- tokens: bfloat16 [4096, 768], P(('dp', 'tensor')), may hold values from -20 to 20
- condition: bfloat16 [16, 768], P('dp'), may hold values from -4 to 4
- adaptive_weight: bfloat16 [768, 6, 768], P('dp', None, 'tensor'), may hold values from -0.21875 to 0.21875
- adaptive_bias: float32 [6, 768], P(None, 'tensor'), may hold values from -3 to 3
- entry_weight: bfloat16 [768, 3, 768], P('dp', None, 'tensor'), may hold values from -1 to 1
- entry_bias: float32 [2, 768], P(None, 'tensor'), may hold values from -3 to 3
- output_weight: bfloat16 [768, 768], P('tensor', 'dp'), may hold values from -0.875 to 0.875
- output_bias: float32 [768], replicated, may hold values from -3 to 3
- expand_weight: bfloat16 [768, 3072], P('dp', 'tensor'), may hold values from -0.21875 to 0.21875
- expand_bias: float32 [3072], P('tensor'), may hold values from -3 to 3
- reduce_weight: bfloat16 [3072, 768], P('tensor', 'dp'), may hold values from -0.109375 to 0.109375
- reduce_bias: float32 [768], replicated, may hold values from -3 to 3
- cotangent: bfloat16 [4096, 768], P(('dp', 'tensor')), may hold values from -6 to 6
Outputs:
- block_output: bfloat16 [4096, 768], P(('dp', 'tensor'))
- tokens_gradient: float32 [4096, 768], P(('dp', 'tensor'))
- condition_gradient: float32 [16, 768], P('dp')
- adaptive_gradient: float32 [768, 6, 768], P('dp', None, 'tensor')
- bias_adaptive: float32 [6, 768], P(None, 'tensor')
- entry_gradient: float32 [768, 3, 768], P('dp', None, 'tensor')
- bias_entry: float32 [2, 768], P(None, 'tensor')
- output_gradient: float32 [768, 768], P('tensor', 'dp')
- bias_output: float32 [768], replicated
- expand_gradient: float32 [768, 3072], P('dp', 'tensor')
- bias_expand: float32 [3072], P('tensor')
- reduce_gradient: float32 [3072, 768], P('tensor', 'dp')
- bias_reduce: float32 [768], replicated
The draws below stay inside these ranges and needn't reach their ends.
All inputs are finite; a program needn't handle non-finite values.
Results may differ from the reference program's by a relative error of at most 0.015.
The reference program's roundings to bfloat16 on the way count: a program that leaves them out, or rounds other values in their place, can miss the bound.
Values may be sent and summed in bfloat16 or wider, within the bound.
A program may use at most 128 MiB of HBM per device.

```python
import math
import jax
import jax.numpy as jnp
from jax import lax

D = 768
HEADS = 12
HEAD_DIM = 64
FF = 3072
LEN = 256
SEQS = 16
TOKENS = 4096


def draw_tokens(key, part):
    key_base, key_scale = jax.random.split(key, 2)
    base = jnp.clip(jax.random.normal(key_base, (SEQS, LEN, D), jnp.float32), -4.0, 4.0)
    row_scale = jnp.exp(jax.random.uniform(key_scale, (SEQS, LEN, 1), jnp.float32, math.log(0.5), math.log(2.0)))
    values = jnp.clip(base * row_scale, -20.0, 20.0)
    return values.reshape(SEQS * LEN, D).astype(jnp.bfloat16)


def draw_entry_weight(key, part):
    key_query, key_noise, key_value = jax.random.split(key, 3)
    root = 1.0 / math.sqrt(D)
    query_part = jax.random.normal(key_query, (D, D), jnp.float32) * root
    key_part = jax.random.normal(key_noise, (D, D), jnp.float32) * root
    value_part = jax.random.normal(key_value, (D, D), jnp.float32) * root
    return jnp.clip(jnp.stack([query_part, key_part, value_part], axis=1), -1.0, 1.0).astype(jnp.bfloat16)


def strengthened(values, rng, source, target, blocks, factor):
    owner, partner = [(jnp.arange(values.shape[axis_at]) // (values.shape[axis_at] // blocks)).reshape([-1 if axis == axis_at else 1 for axis in range(values.ndim)]) for axis_at in (source, target)]
    chosen = jax.random.permutation(rng, blocks)[partner]
    strong = (owner == chosen) | (owner == (partner + blocks // 2) % blocks)
    return jnp.where(strong, factor * values, values)


def levels(rng, dims, cuts, smallest, high):
    level, own = 1.0, jax.random.fold_in(rng, 6)
    for dim, blocks in cuts:
        heights = jnp.exp(jax.random.uniform(jax.random.fold_in(own, dim), (blocks,), jnp.float32, smallest / len(cuts), high / len(cuts)))
        level = level * jnp.repeat(heights, dims[dim] // blocks).reshape([-1 if axis == dim else 1 for axis in range(len(dims))])
    return level


def centred(key, dims, width, reach, shards=(), held_as=jnp.bfloat16):
    values = jax.random.normal(key, dims, jnp.float32) * width
    if len(shards) > 0:
        values = levels(key, dims, shards, -0.22, 0.18) * values
    return jnp.clip(values, min=-reach, max=reach).astype(held_as)


def bell_draw_with(key, shape, spread, reach, cuts, heavy, kind=jnp.bfloat16):
    array = spread * jax.random.normal(key, shape, jnp.float32)
    if cuts:
        array = array * levels(key, shape, cuts, -0.22, 0.18)
    return jnp.clip(strengthened(array, jax.random.fold_in(key, 3), *heavy), -reach, reach).astype(kind)


def setup_inputs(seed: int = 0) -> dict:
    arg_keys = jax.random.split(jax.random.key(seed), 14)
    return {
        "tokens": draw_tokens(jax.random.fold_in(arg_keys[13], 71), 0),
        "condition": centred(arg_keys[1], (SEQS, D), 1.0, 4.0, ((0, 8),)),
        "adaptive_weight": centred(arg_keys[2], (D, 6, D), D ** -0.5, 0.21875, ((0, 8), (2, 4))),
        "adaptive_bias": centred(arg_keys[3], (6, D), 0.5, 3.0, ((1, 4),), jnp.float32),
        "entry_weight": draw_entry_weight(jax.random.fold_in(arg_keys[13], 71), 0),
        "entry_bias": centred(arg_keys[5], (2, D), 0.5, 3.0, ((1, 4),), jnp.float32),
        "output_weight": centred(arg_keys[6], (D, D), (D // 16) ** -0.5, 0.875, ((0, 4), (1, 8))),
        "output_bias": centred(arg_keys[7], (D,), 0.5, 3.0, (), jnp.float32),
        "expand_weight": centred(arg_keys[8], (D, FF), D ** -0.5, 0.21875, ((0, 8), (1, 4))),
        "expand_bias": centred(arg_keys[9], (FF,), 0.5, 3.0, ((0, 4),), jnp.float32),
        "reduce_weight": centred(arg_keys[10], (FF, D), FF ** -0.5, 0.109375, ((0, 4), (1, 8))),
        "reduce_bias": centred(arg_keys[11], (D,), 0.5, 3.0, (), jnp.float32),
        "cotangent": bell_draw_with(arg_keys[12], (TOKENS, D), 1.0, 6.0, ((0, 32),), (0, 1, 32, 2.75)),
    }


NORM_EPSILON = 1e-06
GELU_ROOT = 0.7978845608028654
GELU_CUBIC = 0.044715

def norm_rows(values):
    center = values - lax.optimization_barrier(jnp.mean(values, axis=-1, keepdims=True))
    inverse = lax.rsqrt(lax.optimization_barrier(jnp.mean(center * center, axis=-1, keepdims=True)) + NORM_EPSILON)
    return (center * inverse, inverse)

def norm_back(upstream, normed, inverse):
    return inverse * (upstream - lax.optimization_barrier(jnp.mean(upstream, axis=-1, keepdims=True)) - normed * lax.optimization_barrier(jnp.mean(upstream * normed, axis=-1, keepdims=True)))

def gelu_pair(inputs):
    tangent = jnp.tanh(GELU_ROOT * (inputs + GELU_CUBIC * inputs * inputs * inputs))
    output = 0.5 * inputs * (1.0 + tangent)
    slope_value = 0.5 * (1.0 + tangent) + 0.5 * inputs * (1.0 - tangent * tangent) * GELU_ROOT * (1.0 + 3.0 * GELU_CUBIC * inputs * inputs)
    return (output, slope_value)

def contract_first(left, right):
    return lax.dot_general(left, right, (((0,), (0,)), ((), ())), preferred_element_type=jnp.float32)

def contract_last(left, right):
    return lax.dot_general(left, right, (((1,), (1,)), ((), ())), preferred_element_type=jnp.float32)

def attend(query_rows, key_rows, value_rows):
    factor = query_rows.shape[-1] ** (-0.5)
    scores = jnp.einsum('blhe,bmhe->bhlm', query_rows.astype(jnp.float32), key_rows.astype(jnp.float32)) * factor
    row_top = lax.optimization_barrier(jnp.max(scores, axis=-1, keepdims=True))
    log_total = row_top + jnp.log(lax.optimization_barrier(jnp.sum(jnp.exp(scores - row_top), axis=-1, keepdims=True)))
    weights = jnp.exp(scores - log_total).astype(jnp.bfloat16)
    attended = jnp.einsum('bhlm,bmhe->blhe', weights.astype(jnp.float32), value_rows.astype(jnp.float32))
    return (attended.astype(jnp.bfloat16), log_total)

def attend_back(query_rows, key_rows, value_rows, log_total, attended_grad):
    factor = query_rows.shape[-1] ** (-0.5)
    scores = jnp.einsum('blhe,bmhe->bhlm', query_rows.astype(jnp.float32), key_rows.astype(jnp.float32)) * factor
    probability = jnp.exp(scores - log_total)
    weights = probability.astype(jnp.bfloat16).astype(jnp.float32)
    grad_float = attended_grad.astype(jnp.float32)
    value_grad = jnp.einsum('bhlm,blhe->bmhe', weights, grad_float)
    weight_grad = jnp.einsum('blhe,bmhe->bhlm', grad_float, value_rows.astype(jnp.float32))
    row_inner = lax.optimization_barrier(jnp.sum(probability * weight_grad, axis=-1, keepdims=True))
    score_grad = (probability * (weight_grad - row_inner) * factor).astype(jnp.bfloat16).astype(jnp.float32)
    query_grad = jnp.einsum('bhlm,bmhe->blhe', score_grad, key_rows.astype(jnp.float32))
    key_grad = jnp.einsum('bhlm,blhe->bmhe', score_grad, query_rows.astype(jnp.float32))
    return (query_grad, key_grad, value_grad)

def layer_block(tokens_block, condition_block, cotangent_block, weights):
    adaptive_weight, adaptive_bias, entry_weight, entry_bias, output_weight, output_bias, expand_weight, expand_bias, reduce_weight, reduce_bias = weights
    seq_count = condition_block.shape[0]
    row_total = tokens_block.shape[0]
    condition_float = condition_block.astype(jnp.float32)
    soft_condition = jax.nn.silu(condition_float).astype(jnp.bfloat16)
    modulation = jnp.dot(soft_condition, adaptive_weight.reshape(D, 6 * D), preferred_element_type=jnp.float32).reshape(seq_count, 6, D) + adaptive_bias[None]
    per_row = jnp.repeat(modulation, LEN, axis=0)
    shift_one, scale_one, gate_one, shift_two, scale_two, gate_two = [per_row[:, column] for column in range(6)]
    inputs = tokens_block.astype(jnp.float32)
    normed_one, inverse_one = norm_rows(inputs)
    attention_input = (normed_one * (1.0 + scale_one) + shift_one).astype(jnp.bfloat16)
    projected = jnp.dot(attention_input, entry_weight.reshape(D, 3 * D), preferred_element_type=jnp.float32).reshape(row_total, 3, D)
    head_shape = (seq_count, LEN, HEADS, HEAD_DIM)
    query_rows = (projected[:, 0] + entry_bias[0]).astype(jnp.bfloat16).reshape(head_shape)
    key_rows = projected[:, 1].astype(jnp.bfloat16).reshape(head_shape)
    value_rows = (projected[:, 2] + entry_bias[1]).astype(jnp.bfloat16).reshape(head_shape)
    attended, log_total = attend(query_rows, key_rows, value_rows)
    attended = attended.reshape(row_total, D)
    attention_branch = jnp.dot(attended, output_weight, preferred_element_type=jnp.float32) + output_bias
    middle = inputs + gate_one * attention_branch
    normed_two, inverse_two = norm_rows(middle)
    feed_input = (normed_two * (1.0 + scale_two) + shift_two).astype(jnp.bfloat16)
    hidden_pre = jnp.dot(feed_input, expand_weight, preferred_element_type=jnp.float32) + expand_bias
    hidden_value, hidden_slope = gelu_pair(hidden_pre)
    hidden_rows = hidden_value.astype(jnp.bfloat16)
    feed_branch = jnp.dot(hidden_rows, reduce_weight, preferred_element_type=jnp.float32) + reduce_bias
    block_output = (middle + gate_two * feed_branch).astype(jnp.bfloat16)
    upstream = cotangent_block.astype(jnp.float32)
    feed_grad = upstream * gate_two
    feed_round = feed_grad.astype(jnp.bfloat16)
    reduce_total = contract_first(hidden_rows, feed_round)
    hidden_grad = contract_last(feed_round, reduce_weight) * hidden_slope
    hidden_round = hidden_grad.astype(jnp.bfloat16)
    expand_total = contract_first(feed_input, hidden_round)
    feed_input_grad = contract_last(hidden_round, expand_weight)
    middle_grad = upstream + norm_back(feed_input_grad * (1.0 + scale_two), normed_two, inverse_two)
    attention_grad = middle_grad * gate_one
    attention_round = attention_grad.astype(jnp.bfloat16)
    output_total = contract_first(attended, attention_round)
    attended_grad = contract_last(attention_round, output_weight).astype(jnp.bfloat16).reshape(head_shape)
    query_grad, key_grad, value_grad = attend_back(query_rows, key_rows, value_rows, log_total, attended_grad)
    query_grad = query_grad.reshape(row_total, D)
    key_grad = key_grad.reshape(row_total, D)
    value_grad = value_grad.reshape(row_total, D)
    entry_round = jnp.stack([query_grad, key_grad, value_grad], axis=1).astype(jnp.bfloat16).reshape(row_total, 3 * D)
    entry_total = contract_first(attention_input, entry_round).reshape(D, 3, D)
    input_grad = contract_last(entry_round, entry_weight.reshape(D, 3 * D))
    tokens_gradient = middle_grad + norm_back(input_grad * (1.0 + scale_one), normed_one, inverse_one)
    row_terms = jnp.stack([input_grad, input_grad * normed_one, middle_grad * attention_branch, feed_input_grad, feed_input_grad * normed_two, upstream * feed_branch], axis=1)
    modulation_grad = lax.optimization_barrier(jnp.sum(row_terms.reshape(seq_count, LEN, 6, D), axis=1))
    modulation_round = modulation_grad.astype(jnp.bfloat16).reshape(seq_count, 6 * D)
    adaptive_total = contract_first(soft_condition, modulation_round).reshape(D, 6, D)
    sigmoid_value = jax.nn.sigmoid(condition_float)
    condition_gradient = contract_last(modulation_round, adaptive_weight.reshape(D, 6 * D)) * sigmoid_value * (1.0 + condition_float * (1.0 - sigmoid_value))
    totals = (adaptive_total, lax.optimization_barrier(jnp.sum(modulation_grad, axis=0)), entry_total, jnp.stack([lax.optimization_barrier(jnp.sum(query_grad, axis=0)), lax.optimization_barrier(jnp.sum(value_grad, axis=0))]), output_total, lax.optimization_barrier(jnp.sum(attention_grad, axis=0)), expand_total, lax.optimization_barrier(jnp.sum(hidden_grad, axis=0)), reduce_total, lax.optimization_barrier(jnp.sum(feed_grad, axis=0)))
    return (block_output, tokens_gradient, condition_gradient, totals)

def reference(tokens, condition, adaptive_weight, adaptive_bias, entry_weight, entry_bias, output_weight, output_bias, expand_weight, expand_bias, reduce_weight, reduce_bias, cotangent):
    block_seqs = 16 if SEQS % 16 == 0 else SEQS
    block_count = SEQS // block_seqs
    weights = (adaptive_weight, adaptive_bias, entry_weight, entry_bias, output_weight, output_bias, expand_weight, expand_bias, reduce_weight, reduce_bias)
    token_blocks = tokens.reshape(block_count, block_seqs * LEN, D)
    condition_blocks = condition.reshape(block_count, block_seqs, D)
    cotangent_blocks = cotangent.reshape(block_count, block_seqs * LEN, D)
    zero_totals = tuple((jnp.zeros(member.shape, jnp.float32) for member in weights))

    def step_block(running, block_inputs):
        block_output, tokens_gradient, condition_gradient, totals = layer_block(block_inputs[0], block_inputs[1], block_inputs[2], weights)
        return (jax.tree.map(jnp.add, running, totals), (block_output, tokens_gradient, condition_gradient))
    final_totals, stacked = lax.scan(step_block, zero_totals, (token_blocks, condition_blocks, cotangent_blocks))
    block_output = stacked[0].reshape(TOKENS, D)
    tokens_gradient = stacked[1].reshape(TOKENS, D)
    condition_gradient = stacked[2].reshape(SEQS, D)
    return (block_output, tokens_gradient, condition_gradient, final_totals[0], final_totals[1], final_totals[2], final_totals[3], final_totals[4], final_totals[5], final_totals[6], final_totals[7], final_totals[8], final_totals[9])
```

```python
import jax
import jax.numpy as jnp
from jax import lax
from jax.sharding import PartitionSpec as P

HEAD_DIM = 64
LEN = 256


NORM_EPSILON = 1e-06
GELU_ROOT = 0.7978845608028654
GELU_CUBIC = 0.044715
HIGHEST_PRECISION = lax.Precision.HIGHEST


def norm_rows(values):
    center = values - jnp.mean(values, axis=-1, keepdims=True)
    inverse = lax.rsqrt(jnp.mean(center * center, axis=-1, keepdims=True) + NORM_EPSILON)
    return (center * inverse, inverse)


def norm_back(upstream, normed, inverse):
    return inverse * (
        upstream
        - jnp.mean(upstream, axis=-1, keepdims=True)
        - normed * jnp.mean(upstream * normed, axis=-1, keepdims=True)
    )


def gelu_pair(inputs):
    tangent = jnp.tanh(GELU_ROOT * (inputs + GELU_CUBIC * inputs * inputs * inputs))
    output = 0.5 * inputs * (1.0 + tangent)
    slope_value = 0.5 * (1.0 + tangent) + 0.5 * inputs * (1.0 - tangent * tangent) * GELU_ROOT * (
        1.0 + 3.0 * GELU_CUBIC * inputs * inputs
    )
    return (output, slope_value)


def contract_first(left, right):
    return lax.dot_general(
        left, right, (((0,), (0,)), ((), ())), preferred_element_type=jnp.float32
    )


def contract_last(left, right):
    return lax.dot_general(
        left, right, (((1,), (1,)), ((), ())), preferred_element_type=jnp.float32
    )


def gather_rows(values):
    return lax.all_gather(values, "tensor", axis=0, tiled=True)


def sum_rows(values):
    return lax.psum_scatter(
        values.astype(jnp.bfloat16), "tensor", scatter_dimension=0, tiled=True
    ).astype(jnp.float32)


def gather_weights(shards):
    return [lax.all_gather(shard, "dp", axis=0, tiled=True) for shard in shards]


def scatter_gradients(totals):
    return [
        lax.psum_scatter(
            total.astype(jnp.bfloat16), "dp", scatter_dimension=0, tiled=True
        ).astype(jnp.float32)
        for total in totals
    ]


def attend(query_rows, key_rows, value_rows):
    factor = query_rows.shape[-1] ** (-0.5)
    scores = (
        jnp.einsum("blhe,bmhe->bhlm", query_rows, key_rows, preferred_element_type=jnp.float32)
        * factor
    )
    row_top = jnp.max(scores, axis=-1, keepdims=True)
    log_total = row_top + jnp.log(jnp.sum(jnp.exp(scores - row_top), axis=-1, keepdims=True))
    weights = jnp.exp(scores - log_total).astype(jnp.bfloat16)
    attended = jnp.einsum(
        "bhlm,bmhe->blhe", weights, value_rows, preferred_element_type=jnp.float32
    )
    return (attended.astype(jnp.bfloat16), log_total)


def attend_back(query_rows, key_rows, value_rows, log_total, attended_grad):
    factor = query_rows.shape[-1] ** (-0.5)
    scores = (
        jnp.einsum("blhe,bmhe->bhlm", query_rows, key_rows, preferred_element_type=jnp.float32)
        * factor
    )
    probability = jnp.exp(scores - log_total)
    weights = probability.astype(jnp.bfloat16)
    value_grad = jnp.einsum(
        "bhlm,blhe->bmhe", weights, attended_grad, preferred_element_type=jnp.float32
    )
    weight_grad = jnp.einsum(
        "blhe,bmhe->bhlm", attended_grad, value_rows, preferred_element_type=jnp.float32
    )
    row_inner = jnp.sum(probability * weight_grad, axis=-1, keepdims=True)
    score_grad = (probability * (weight_grad - row_inner) * factor).astype(jnp.bfloat16)
    query_grad = jnp.einsum(
        "bhlm,bmhe->blhe", score_grad, key_rows, preferred_element_type=jnp.float32
    )
    key_grad = jnp.einsum(
        "bhlm,blhe->bmhe", score_grad, query_rows, preferred_element_type=jnp.float32
    )
    return (query_grad, key_grad, value_grad)


def body(
    tokens,
    condition,
    adaptive_weight,
    adaptive_bias,
    entry_weight,
    entry_bias,
    output_weight,
    output_bias,
    expand_weight,
    expand_bias,
    reduce_weight,
    reduce_bias,
    cotangent,
):
    tensor_index = lax.axis_index("tensor")
    tensor_count = lax.axis_size("tensor")
    row_count = tokens.shape[0]
    features = tokens.shape[1]
    seq_count = condition.shape[0]
    local_width = adaptive_bias.shape[1]
    local_hidden = expand_bias.shape[0]
    group_rows = row_count * tensor_count
    head_count = local_width // HEAD_DIM
    head_shape = (seq_count, LEN, head_count, HEAD_DIM)
    dp_index = lax.axis_index("dp")
    dp_count = lax.axis_size("dp")
    shard_rows = adaptive_weight.shape[0]
    entry_flat = entry_weight.reshape(shard_rows, 3 * local_width)
    entry_full, output_full, expand_full, reduce_full = gather_weights(
        (entry_flat, output_weight.T, expand_weight, reduce_weight.T)
    )
    condition_float = condition.astype(jnp.float32)
    condition_all = lax.all_gather(condition, "dp", axis=0, tiled=True)
    soft_all = jax.nn.silu(condition_all.astype(jnp.float32)).astype(jnp.bfloat16)
    soft_mine = lax.dynamic_slice_in_dim(soft_all, dp_index * shard_rows, shard_rows, 1)
    adaptive_flat = adaptive_weight.reshape(shard_rows, 6 * local_width)
    modulation_partial = jnp.dot(soft_mine, adaptive_flat, preferred_element_type=jnp.float32)
    modulation_local = (
        lax.psum_scatter(modulation_partial, "dp", scatter_dimension=0, tiled=True).reshape(
            seq_count, 6, local_width
        )
        + adaptive_bias[None]
    )
    modulation = lax.all_gather(modulation_local, "tensor", axis=2, tiled=True)
    seq_of_row = (tensor_index * row_count + jnp.arange(row_count, dtype=jnp.int32)) // LEN
    selector = (seq_of_row[:, None] == jnp.arange(seq_count, dtype=jnp.int32)[None, :]).astype(
        jnp.float32
    )
    per_row = jnp.dot(
        selector, modulation.reshape(seq_count, 6 * features), precision=HIGHEST_PRECISION
    ).reshape(row_count, 6, features)
    shift_one, scale_one, gate_one, shift_two, scale_two, gate_two = [
        per_row[:, column] for column in range(6)
    ]
    inputs = tokens.astype(jnp.float32)
    normed_one, inverse_one = norm_rows(inputs)
    attention_local = (normed_one * (1.0 + scale_one) + shift_one).astype(jnp.bfloat16)
    attention_input = gather_rows(attention_local)
    projected = jnp.dot(
        attention_input,
        entry_full,
        preferred_element_type=jnp.float32,
    ).reshape(group_rows, 3, local_width)
    query_rows = (projected[:, 0] + entry_bias[0]).astype(jnp.bfloat16).reshape(head_shape)
    key_rows = projected[:, 1].astype(jnp.bfloat16).reshape(head_shape)
    value_rows = (projected[:, 2] + entry_bias[1]).astype(jnp.bfloat16).reshape(head_shape)
    attended, log_total = attend(query_rows, key_rows, value_rows)
    attended = attended.reshape(group_rows, local_width)
    attention_branch = (
        sum_rows(contract_last(attended, output_full)) + output_bias
    )
    middle = inputs + gate_one * attention_branch
    normed_two, inverse_two = norm_rows(middle)
    feed_local = (normed_two * (1.0 + scale_two) + shift_two).astype(jnp.bfloat16)
    feed_input = gather_rows(feed_local)
    hidden_pre = jnp.dot(feed_input, expand_full, preferred_element_type=jnp.float32) + expand_bias
    hidden_value, hidden_slope = gelu_pair(hidden_pre)
    hidden_rows = hidden_value.astype(jnp.bfloat16)
    feed_branch = (
        sum_rows(contract_last(hidden_rows, reduce_full))
        + reduce_bias
    )
    block_output = (middle + gate_two * feed_branch).astype(jnp.bfloat16)
    upstream = cotangent.astype(jnp.float32)
    feed_grad = upstream * gate_two
    feed_gathered = gather_rows(feed_grad.astype(jnp.bfloat16))
    reduce_total = contract_first(feed_gathered, hidden_rows)
    hidden_grad = jnp.dot(feed_gathered, reduce_full, preferred_element_type=jnp.float32) * hidden_slope
    hidden_round = hidden_grad.astype(jnp.bfloat16)
    expand_total = contract_first(feed_input, hidden_round)
    feed_input_grad = sum_rows(contract_last(hidden_round, expand_full))
    middle_grad = upstream + norm_back(feed_input_grad * (1.0 + scale_two), normed_two, inverse_two)
    attention_grad = middle_grad * gate_one
    attention_gathered = gather_rows(attention_grad.astype(jnp.bfloat16))
    output_total = contract_first(attention_gathered, attended)
    attended_grad = (
        jnp.dot(attention_gathered, output_full, preferred_element_type=jnp.float32)
        .astype(jnp.bfloat16)
        .reshape(head_shape)
    )
    query_grad, key_grad, value_grad = attend_back(
        query_rows, key_rows, value_rows, log_total, attended_grad
    )
    query_grad = query_grad.reshape(group_rows, local_width)
    key_grad = key_grad.reshape(group_rows, local_width)
    value_grad = value_grad.reshape(group_rows, local_width)
    entry_round = (
        jnp.stack([query_grad, key_grad, value_grad], axis=1)
        .astype(jnp.bfloat16)
        .reshape(group_rows, 3 * local_width)
    )
    entry_total = contract_first(attention_input, entry_round)
    input_grad = sum_rows(contract_last(entry_round, entry_full))
    tokens_gradient = middle_grad + norm_back(
        input_grad * (1.0 + scale_one), normed_one, inverse_one
    )
    row_terms = jnp.stack(
        [
            input_grad,
            input_grad * normed_one,
            middle_grad * attention_branch,
            feed_input_grad,
            feed_input_grad * normed_two,
            upstream * feed_branch,
        ],
        axis=1,
    )
    per_sequence = lax.dot_general(
        selector,
        row_terms.reshape(row_count, 6 * features),
        (((0,), (0,)), ((), ())),
        precision=HIGHEST_PRECISION,
        preferred_element_type=jnp.float32,
    ).reshape(seq_count, 6, features)
    modulation_grad = lax.psum_scatter(
        per_sequence.astype(jnp.bfloat16), "tensor", scatter_dimension=2, tiled=True
    ).astype(jnp.float32)
    modulation_all = lax.all_gather(
        modulation_grad.reshape(seq_count, 6 * local_width), "dp", axis=0, tiled=True
    )
    bias_adaptive = jnp.sum(modulation_all, axis=0).reshape(6, local_width)
    modulation_round = modulation_all.astype(jnp.bfloat16)
    adaptive_gradient = contract_first(soft_mine, modulation_round).reshape(
        shard_rows, 6, local_width
    )
    condition_partial = contract_last(modulation_round, adaptive_flat)
    condition_moved = lax.all_to_all(
        condition_partial.reshape(dp_count, seq_count, shard_rows), "dp", 0, 0
    )
    condition_sum = lax.psum(
        condition_moved.transpose(1, 0, 2).reshape(seq_count, features), "tensor"
    )
    sigmoid_value = jax.nn.sigmoid(condition_float)
    condition_gradient = (
        condition_sum * sigmoid_value * (1.0 + condition_float * (1.0 - sigmoid_value))
    )
    entry_gradient, output_gradient, expand_gradient, reduce_gradient = scatter_gradients(
        (entry_total, output_total, expand_total, reduce_total)
    )
    entry_gradient = entry_gradient.reshape(shard_rows, 3, local_width)
    output_gradient = output_gradient.T
    reduce_gradient = reduce_gradient.T
    own_sums = jnp.concatenate(
        [
            jnp.sum(query_grad, axis=0),
            jnp.sum(value_grad, axis=0),
            jnp.sum(hidden_grad, axis=0),
            jnp.sum(attention_grad, axis=0),
            jnp.sum(feed_grad, axis=0),
        ]
    )
    dp_sums = lax.psum(own_sums, "dp")
    own_width = 2 * local_width + local_hidden
    bias_entry = dp_sums[: 2 * local_width].reshape(2, local_width)
    bias_expand = dp_sums[2 * local_width : own_width]
    row_sums = lax.psum(dp_sums[own_width:], "tensor")
    output_sums = row_sums[:features]
    reduce_sums = row_sums[features:]
    return (
        block_output,
        tokens_gradient,
        condition_gradient,
        adaptive_gradient,
        bias_adaptive,
        entry_gradient,
        bias_entry,
        output_gradient,
        output_sums,
        expand_gradient,
        bias_expand,
        reduce_gradient,
        reduce_sums,
    )


def solution(mesh):
    in_specs = (
        P(("dp", "tensor"), None),
        P("dp", None),
        P("dp", None, "tensor"),
        P(None, "tensor"),
        P("dp", None, "tensor"),
        P(None, "tensor"),
        P("tensor", "dp"),
        P(),
        P("dp", "tensor"),
        P("tensor"),
        P("tensor", "dp"),
        P(),
        P(("dp", "tensor"), None),
    )
    out_specs = (
        P(("dp", "tensor"), None),
        P(("dp", "tensor"), None),
        P("dp", None),
        P("dp", None, "tensor"),
        P(None, "tensor"),
        P("dp", None, "tensor"),
        P(None, "tensor"),
        P("tensor", "dp"),
        P(),
        P("dp", "tensor"),
        P("tensor"),
        P("tensor", "dp"),
        P(),
    )
    return jax.shard_map(body, mesh=mesh, in_specs=in_specs, out_specs=out_specs, check_vma=False)
```

```python
import functools

import jax
import jax.numpy as jnp
from jax import lax
from jax.experimental import pallas as pl
from jax.experimental.pallas import tpu as pltpu
from jax.sharding import PartitionSpec as P

HEAD_DIM = 64
LEN = 256


NORM_EPSILON = 1e-06
GELU_ROOT = 0.7978845608028654
GELU_CUBIC = 0.044715
HIGHEST_PRECISION = lax.Precision.HIGHEST


def norm_rows(values):
    center = values - jnp.mean(values, axis=-1, keepdims=True)
    inverse = lax.rsqrt(jnp.mean(center * center, axis=-1, keepdims=True) + NORM_EPSILON)
    return (center * inverse, inverse)


def norm_back(upstream, normed, inverse):
    return inverse * (
        upstream
        - jnp.mean(upstream, axis=-1, keepdims=True)
        - normed * jnp.mean(upstream * normed, axis=-1, keepdims=True)
    )


def gelu_pair(inputs):
    tangent = jnp.tanh(GELU_ROOT * (inputs + GELU_CUBIC * inputs * inputs * inputs))
    output = 0.5 * inputs * (1.0 + tangent)
    slope_value = 0.5 * (1.0 + tangent) + 0.5 * inputs * (1.0 - tangent * tangent) * GELU_ROOT * (
        1.0 + 3.0 * GELU_CUBIC * inputs * inputs
    )
    return (output, slope_value)


def contract_first(left, right):
    return lax.dot_general(
        left, right, (((0,), (0,)), ((), ())), preferred_element_type=jnp.float32
    )


def contract_last(left, right):
    return lax.dot_general(
        left, right, (((1,), (1,)), ((), ())), preferred_element_type=jnp.float32
    )


def gather_rows(values):
    return lax.all_gather(values, "tensor", axis=0, tiled=True)


def sum_rows(values):
    return lax.psum_scatter(
        values.astype(jnp.bfloat16), "tensor", scatter_dimension=0, tiled=True
    ).astype(jnp.float32)


MESH = pl.DeviceIdType.MESH
ANY = pl.BlockSpec(memory_space=pl.ANY)
VMEM = pl.BlockSpec(memory_space=pltpu.VMEM)
PAIR = 2


def greet(position, length, mate, below, above):
    barrier = pltpu.get_barrier_semaphore()
    pl.semaphore_signal(barrier, inc=1, device_id=mate, device_id_type=MESH)

    @pl.when(position > 0)
    def _():
        pl.semaphore_signal(barrier, inc=1, device_id=below, device_id_type=MESH)

    @pl.when(position < length - 1)
    def _():
        pl.semaphore_signal(barrier, inc=1, device_id=above, device_id_type=MESH)

    inner = jnp.minimum(position, 1) + jnp.minimum(length - 1 - position, 1)
    pl.semaphore_wait(barrier, 1 + inner)


def places(length):
    me = lax.axis_index("dp")
    column = lax.axis_index("tensor")
    position, side = me // PAIR, me % PAIR
    mate = (position * PAIR + 1 - side, column)
    below = (jnp.maximum(me - PAIR, 0), column)
    above = (jnp.minimum(me + PAIR, length * PAIR - 1), column)
    return position, side, mate, below, above


def gather_kernel(length, count, *refs):
    ins, outs = refs[:count], refs[count : 2 * count]
    own_sem, send_sem, recv_sem = refs[2 * count :]
    position, side, mate, below, above = places(length)
    greet(position, length, mate, below, above)

    def copy(way, item, shard, target, source=None):
        place = outs[item].at[shard * PAIR + side]
        return pltpu.make_async_remote_copy(
            src_ref=place if source is None else source,
            dst_ref=place,
            send_sem=send_sem.at[way, item, shard],
            recv_sem=recv_sem.at[way, item, shard],
            device_id=target,
            device_id_type=MESH,
        )

    def own(item):
        return pltpu.make_async_copy(
            ins[item], outs[item].at[position * PAIR + side], own_sem.at[item]
        )

    for item in range(count):
        own(item).start()
    for step in range(length):
        for item in range(count):
            source = ins[item] if step == 0 else None
            low = position - step
            high = position + step

            @pl.when(low >= 0)
            def _(item=item, low=low, source=source, step=step):
                if step > 0:
                    copy(0, item, low, above).wait_recv()

                @pl.when(position < length - 1)
                def _():
                    copy(0, item, low, above, source).start()

                copy(2, item, low, mate, source).start()

            @pl.when(high < length)
            def _(item=item, high=high, source=source, step=step):
                if step > 0:
                    copy(1, item, high, below).wait_recv()

                @pl.when(position > 0)
                def _():
                    copy(1, item, high, below, source).start()

                if step > 0:
                    copy(2, item, high, mate).start()

    for item in range(count):
        own(item).wait()
        for shard in range(length):
            place = outs[item].at[shard * PAIR + 1 - side]
            pltpu.make_async_remote_copy(
                src_ref=place,
                dst_ref=place,
                send_sem=send_sem.at[2, item, shard],
                recv_sem=recv_sem.at[2, item, shard],
                device_id=mate,
                device_id_type=MESH,
            ).wait_recv()
            copy(2, item, shard, mate).wait_send()

            @pl.when((shard <= position) & (position < length - 1))
            def _(item=item, shard=shard):
                copy(0, item, shard, above).wait_send()

            @pl.when((shard >= position) & (position > 0))
            def _(item=item, shard=shard):
                copy(1, item, shard, below).wait_send()


def gather_weights(shards):
    dp_count = lax.axis_size("dp")
    length, count = dp_count // PAIR, len(shards)
    gathered = pl.pallas_call(
        functools.partial(gather_kernel, length, count),
        out_shape=[jax.ShapeDtypeStruct((dp_count,) + s.shape, s.dtype) for s in shards],
        in_specs=[ANY] * count,
        out_specs=[ANY] * count,
        scratch_shapes=[
            pltpu.SemaphoreType.DMA((count,)),
            pltpu.SemaphoreType.DMA((3, count, length)),
            pltpu.SemaphoreType.DMA((3, count, length)),
        ],
        compiler_params=pltpu.CompilerParams(collective_id=0, has_side_effects=True),
    )(*shards)
    return [g.reshape(dp_count * g.shape[1], g.shape[2]) for g in gathered]


def scatter_kernel(length, count, *refs):
    ins, outs = refs[:count], refs[count : 2 * count]
    swap_refs = refs[2 * count : 3 * count]
    sent_refs = refs[3 * count : 4 * count]
    line_refs = refs[4 * count : 5 * count]
    send_sem, recv_sem = refs[5 * count :]
    position, side, mate, below, above = places(length)
    greet(position, length, mate, below, above)
    order = []
    for step in range(length):
        for target in (length - 1 - step, step):
            if target not in order:
                order.append(target)

    def swap(item, target):
        return pltpu.make_async_remote_copy(
            src_ref=ins[item].at[target * PAIR + 1 - side],
            dst_ref=swap_refs[item].at[target],
            send_sem=send_sem.at[2, item, target],
            recv_sem=recv_sem.at[2, item, target],
            device_id=mate,
            device_id_type=MESH,
        )

    def hop(way, item, target):
        return pltpu.make_async_remote_copy(
            src_ref=sent_refs[item].at[target],
            dst_ref=line_refs[item].at[way, target],
            send_sem=send_sem.at[way, item, target],
            recv_sem=recv_sem.at[way, item, target],
            device_id=above if way == 0 else below,
            device_id_type=MESH,
        )

    def paired(item, target):
        swap(item, target).wait_recv()
        mine = ins[item][target * PAIR + side].astype(jnp.float32)
        return mine + swap_refs[item][target].astype(jnp.float32)

    for target in order:
        for item in range(count):
            swap(item, target).start()
    for target in order:
        for item in range(count):
            for way, passes, inner in (
                (0, position < target, position > 0),
                (1, position > target, position < length - 1),
            ):

                @pl.when(passes)
                def _(way=way, inner=inner, item=item, target=target):
                    kind = sent_refs[item].dtype

                    @pl.when(inner)
                    def _():
                        hop(way, item, target).wait_recv()
                        total = paired(item, target) + line_refs[item][way, target].astype(
                            jnp.float32
                        )
                        sent_refs[item][target] = total.astype(kind)

                    @pl.when(jnp.logical_not(inner))
                    def _():
                        sent_refs[item][target] = paired(item, target).astype(kind)

                    hop(way, item, target).start()

    for item in range(count):
        for target in range(length):

            @pl.when(position == target)
            def _(item=item, target=target):
                outs[item][...] = paired(item, target)
                if target > 0:
                    hop(0, item, target).wait_recv()
                    outs[item][...] += line_refs[item][0, target].astype(jnp.float32)
                if target < length - 1:
                    hop(1, item, target).wait_recv()
                    outs[item][...] += line_refs[item][1, target].astype(jnp.float32)

            @pl.when(position < target)
            def _(item=item, target=target):
                hop(0, item, target).wait_send()

            @pl.when(position > target)
            def _(item=item, target=target):
                hop(1, item, target).wait_send()

            swap(item, target).wait_send()


def scatter_gradients(totals):
    dp_count = lax.axis_size("dp")
    length, count = dp_count // PAIR, len(totals)
    kind = jnp.bfloat16
    parts = [t.astype(kind).reshape(dp_count, t.shape[0] // dp_count, t.shape[1]) for t in totals]
    shapes = [p.shape[1:] for p in parts]
    return pl.pallas_call(
        functools.partial(scatter_kernel, length, count),
        out_shape=[jax.ShapeDtypeStruct(s, jnp.float32) for s in shapes],
        in_specs=[VMEM] * count,
        out_specs=[VMEM] * count,
        scratch_shapes=[pltpu.VMEM((length,) + s, kind) for s in shapes]
        + [pltpu.VMEM((length,) + s, kind) for s in shapes]
        + [pltpu.VMEM((2, length) + s, kind) for s in shapes]
        + [
            pltpu.SemaphoreType.DMA((3, count, length)),
            pltpu.SemaphoreType.DMA((3, count, length)),
        ],
        compiler_params=pltpu.CompilerParams(collective_id=1, has_side_effects=True),
    )(*parts)


def attend(query_rows, key_rows, value_rows):
    factor = query_rows.shape[-1] ** (-0.5)
    scores = (
        jnp.einsum("blhe,bmhe->bhlm", query_rows, key_rows, preferred_element_type=jnp.float32)
        * factor
    )
    row_top = jnp.max(scores, axis=-1, keepdims=True)
    log_total = row_top + jnp.log(jnp.sum(jnp.exp(scores - row_top), axis=-1, keepdims=True))
    weights = jnp.exp(scores - log_total).astype(jnp.bfloat16)
    attended = jnp.einsum(
        "bhlm,bmhe->blhe", weights, value_rows, preferred_element_type=jnp.float32
    )
    return (attended.astype(jnp.bfloat16), log_total)


def attend_back(query_rows, key_rows, value_rows, log_total, attended_grad):
    factor = query_rows.shape[-1] ** (-0.5)
    scores = (
        jnp.einsum("blhe,bmhe->bhlm", query_rows, key_rows, preferred_element_type=jnp.float32)
        * factor
    )
    probability = jnp.exp(scores - log_total)
    weights = probability.astype(jnp.bfloat16)
    value_grad = jnp.einsum(
        "bhlm,blhe->bmhe", weights, attended_grad, preferred_element_type=jnp.float32
    )
    weight_grad = jnp.einsum(
        "blhe,bmhe->bhlm", attended_grad, value_rows, preferred_element_type=jnp.float32
    )
    row_inner = jnp.sum(probability * weight_grad, axis=-1, keepdims=True)
    score_grad = (probability * (weight_grad - row_inner) * factor).astype(jnp.bfloat16)
    query_grad = jnp.einsum(
        "bhlm,bmhe->blhe", score_grad, key_rows, preferred_element_type=jnp.float32
    )
    key_grad = jnp.einsum(
        "bhlm,blhe->bmhe", score_grad, query_rows, preferred_element_type=jnp.float32
    )
    return (query_grad, key_grad, value_grad)


def body(
    tokens,
    condition,
    adaptive_weight,
    adaptive_bias,
    entry_weight,
    entry_bias,
    output_weight,
    output_bias,
    expand_weight,
    expand_bias,
    reduce_weight,
    reduce_bias,
    cotangent,
):
    tensor_index = lax.axis_index("tensor")
    tensor_count = lax.axis_size("tensor")
    row_count = tokens.shape[0]
    features = tokens.shape[1]
    seq_count = condition.shape[0]
    local_width = adaptive_bias.shape[1]
    local_hidden = expand_bias.shape[0]
    group_rows = row_count * tensor_count
    head_count = local_width // HEAD_DIM
    head_shape = (seq_count, LEN, head_count, HEAD_DIM)
    dp_index = lax.axis_index("dp")
    dp_count = lax.axis_size("dp")
    shard_rows = adaptive_weight.shape[0]
    entry_flat = entry_weight.reshape(shard_rows, 3 * local_width)
    entry_full, output_full, expand_full, reduce_full = gather_weights(
        (entry_flat, output_weight.T, expand_weight, reduce_weight.T)
    )
    condition_float = condition.astype(jnp.float32)
    condition_all = lax.all_gather(condition, "dp", axis=0, tiled=True)
    soft_all = jax.nn.silu(condition_all.astype(jnp.float32)).astype(jnp.bfloat16)
    soft_mine = lax.dynamic_slice_in_dim(soft_all, dp_index * shard_rows, shard_rows, 1)
    adaptive_flat = adaptive_weight.reshape(shard_rows, 6 * local_width)
    modulation_partial = jnp.dot(soft_mine, adaptive_flat, preferred_element_type=jnp.float32)
    modulation_local = (
        lax.psum_scatter(modulation_partial, "dp", scatter_dimension=0, tiled=True).reshape(
            seq_count, 6, local_width
        )
        + adaptive_bias[None]
    )
    modulation = lax.all_gather(modulation_local, "tensor", axis=2, tiled=True)
    seq_of_row = (tensor_index * row_count + jnp.arange(row_count, dtype=jnp.int32)) // LEN
    selector = (seq_of_row[:, None] == jnp.arange(seq_count, dtype=jnp.int32)[None, :]).astype(
        jnp.float32
    )
    per_row = jnp.dot(
        selector, modulation.reshape(seq_count, 6 * features), precision=HIGHEST_PRECISION
    ).reshape(row_count, 6, features)
    shift_one, scale_one, gate_one, shift_two, scale_two, gate_two = [
        per_row[:, column] for column in range(6)
    ]
    inputs = tokens.astype(jnp.float32)
    normed_one, inverse_one = norm_rows(inputs)
    attention_local = (normed_one * (1.0 + scale_one) + shift_one).astype(jnp.bfloat16)
    attention_input = gather_rows(attention_local)
    projected = jnp.dot(
        attention_input,
        entry_full,
        preferred_element_type=jnp.float32,
    ).reshape(group_rows, 3, local_width)
    query_rows = (projected[:, 0] + entry_bias[0]).astype(jnp.bfloat16).reshape(head_shape)
    key_rows = projected[:, 1].astype(jnp.bfloat16).reshape(head_shape)
    value_rows = (projected[:, 2] + entry_bias[1]).astype(jnp.bfloat16).reshape(head_shape)
    attended, log_total = attend(query_rows, key_rows, value_rows)
    attended = attended.reshape(group_rows, local_width)
    attention_branch = (
        sum_rows(contract_last(attended, output_full)) + output_bias
    )
    middle = inputs + gate_one * attention_branch
    normed_two, inverse_two = norm_rows(middle)
    feed_local = (normed_two * (1.0 + scale_two) + shift_two).astype(jnp.bfloat16)
    feed_input = gather_rows(feed_local)
    hidden_pre = jnp.dot(feed_input, expand_full, preferred_element_type=jnp.float32) + expand_bias
    hidden_value, hidden_slope = gelu_pair(hidden_pre)
    hidden_rows = hidden_value.astype(jnp.bfloat16)
    feed_branch = (
        sum_rows(contract_last(hidden_rows, reduce_full))
        + reduce_bias
    )
    block_output = (middle + gate_two * feed_branch).astype(jnp.bfloat16)
    upstream = cotangent.astype(jnp.float32)
    feed_grad = upstream * gate_two
    feed_gathered = gather_rows(feed_grad.astype(jnp.bfloat16))
    reduce_total = contract_first(feed_gathered, hidden_rows)
    hidden_grad = jnp.dot(feed_gathered, reduce_full, preferred_element_type=jnp.float32) * hidden_slope
    hidden_round = hidden_grad.astype(jnp.bfloat16)
    expand_total = contract_first(feed_input, hidden_round)
    feed_input_grad = sum_rows(contract_last(hidden_round, expand_full))
    middle_grad = upstream + norm_back(feed_input_grad * (1.0 + scale_two), normed_two, inverse_two)
    attention_grad = middle_grad * gate_one
    attention_gathered = gather_rows(attention_grad.astype(jnp.bfloat16))
    output_total = contract_first(attention_gathered, attended)
    attended_grad = (
        jnp.dot(attention_gathered, output_full, preferred_element_type=jnp.float32)
        .astype(jnp.bfloat16)
        .reshape(head_shape)
    )
    query_grad, key_grad, value_grad = attend_back(
        query_rows, key_rows, value_rows, log_total, attended_grad
    )
    query_grad = query_grad.reshape(group_rows, local_width)
    key_grad = key_grad.reshape(group_rows, local_width)
    value_grad = value_grad.reshape(group_rows, local_width)
    entry_round = (
        jnp.stack([query_grad, key_grad, value_grad], axis=1)
        .astype(jnp.bfloat16)
        .reshape(group_rows, 3 * local_width)
    )
    entry_total = contract_first(attention_input, entry_round)
    input_grad = sum_rows(contract_last(entry_round, entry_full))
    tokens_gradient = middle_grad + norm_back(
        input_grad * (1.0 + scale_one), normed_one, inverse_one
    )
    row_terms = jnp.stack(
        [
            input_grad,
            input_grad * normed_one,
            middle_grad * attention_branch,
            feed_input_grad,
            feed_input_grad * normed_two,
            upstream * feed_branch,
        ],
        axis=1,
    )
    per_sequence = lax.dot_general(
        selector,
        row_terms.reshape(row_count, 6 * features),
        (((0,), (0,)), ((), ())),
        precision=HIGHEST_PRECISION,
        preferred_element_type=jnp.float32,
    ).reshape(seq_count, 6, features)
    modulation_grad = lax.psum_scatter(
        per_sequence.astype(jnp.bfloat16), "tensor", scatter_dimension=2, tiled=True
    ).astype(jnp.float32)
    modulation_all = lax.all_gather(
        modulation_grad.reshape(seq_count, 6 * local_width), "dp", axis=0, tiled=True
    )
    bias_adaptive = jnp.sum(modulation_all, axis=0).reshape(6, local_width)
    modulation_round = modulation_all.astype(jnp.bfloat16)
    adaptive_gradient = contract_first(soft_mine, modulation_round).reshape(
        shard_rows, 6, local_width
    )
    condition_partial = contract_last(modulation_round, adaptive_flat)
    condition_moved = lax.all_to_all(
        condition_partial.reshape(dp_count, seq_count, shard_rows), "dp", 0, 0
    )
    condition_sum = lax.psum(
        condition_moved.transpose(1, 0, 2).reshape(seq_count, features), "tensor"
    )
    sigmoid_value = jax.nn.sigmoid(condition_float)
    condition_gradient = (
        condition_sum * sigmoid_value * (1.0 + condition_float * (1.0 - sigmoid_value))
    )
    entry_gradient, output_gradient, expand_gradient, reduce_gradient = scatter_gradients(
        (entry_total, output_total, expand_total, reduce_total)
    )
    entry_gradient = entry_gradient.reshape(shard_rows, 3, local_width)
    output_gradient = output_gradient.T
    reduce_gradient = reduce_gradient.T
    own_sums = jnp.concatenate(
        [
            jnp.sum(query_grad, axis=0),
            jnp.sum(value_grad, axis=0),
            jnp.sum(hidden_grad, axis=0),
            jnp.sum(attention_grad, axis=0),
            jnp.sum(feed_grad, axis=0),
        ]
    )
    dp_sums = lax.psum(own_sums, "dp")
    own_width = 2 * local_width + local_hidden
    bias_entry = dp_sums[: 2 * local_width].reshape(2, local_width)
    bias_expand = dp_sums[2 * local_width : own_width]
    row_sums = lax.psum(dp_sums[own_width:], "tensor")
    output_sums = row_sums[:features]
    reduce_sums = row_sums[features:]
    return (
        block_output,
        tokens_gradient,
        condition_gradient,
        adaptive_gradient,
        bias_adaptive,
        entry_gradient,
        bias_entry,
        output_gradient,
        output_sums,
        expand_gradient,
        bias_expand,
        reduce_gradient,
        reduce_sums,
    )


def solution(mesh):
    in_specs = (
        P(("dp", "tensor"), None),
        P("dp", None),
        P("dp", None, "tensor"),
        P(None, "tensor"),
        P("dp", None, "tensor"),
        P(None, "tensor"),
        P("tensor", "dp"),
        P(),
        P("dp", "tensor"),
        P("tensor"),
        P("tensor", "dp"),
        P(),
        P(("dp", "tensor"), None),
    )
    out_specs = (
        P(("dp", "tensor"), None),
        P(("dp", "tensor"), None),
        P("dp", None),
        P("dp", None, "tensor"),
        P(None, "tensor"),
        P("dp", None, "tensor"),
        P(None, "tensor"),
        P("tensor", "dp"),
        P(),
        P("dp", "tensor"),
        P("tensor"),
        P("tensor", "dp"),
        P(),
    )
    return jax.shard_map(body, mesh=mesh, in_specs=in_specs, out_specs=out_specs, check_vma=False)
```

```python
import functools

import jax
import jax.numpy as jnp
from jax import lax
from jax.experimental import pallas as pl
from jax.experimental.pallas import tpu as pltpu
from jax.sharding import PartitionSpec as P

HEAD_DIM = 64
LEN = 256


NORM_EPSILON = 1e-06
GELU_ROOT = 0.7978845608028654
GELU_CUBIC = 0.044715
HIGHEST_PRECISION = lax.Precision.HIGHEST


def norm_rows(values):
    center = values - jnp.mean(values, axis=-1, keepdims=True)
    inverse = lax.rsqrt(jnp.mean(center * center, axis=-1, keepdims=True) + NORM_EPSILON)
    return (center * inverse, inverse)


def norm_back(upstream, normed, inverse):
    return inverse * (
        upstream
        - jnp.mean(upstream, axis=-1, keepdims=True)
        - normed * jnp.mean(upstream * normed, axis=-1, keepdims=True)
    )


def gelu_pair(inputs):
    tangent = jnp.tanh(GELU_ROOT * (inputs + GELU_CUBIC * inputs * inputs * inputs))
    output = 0.5 * inputs * (1.0 + tangent)
    slope_value = 0.5 * (1.0 + tangent) + 0.5 * inputs * (1.0 - tangent * tangent) * GELU_ROOT * (
        1.0 + 3.0 * GELU_CUBIC * inputs * inputs
    )
    return (output, slope_value)


def contract_first(left, right):
    return lax.dot_general(
        left, right, (((0,), (0,)), ((), ())), preferred_element_type=jnp.float32
    )


def contract_last(left, right):
    return lax.dot_general(
        left, right, (((1,), (1,)), ((), ())), preferred_element_type=jnp.float32
    )


def gather_rows(values):
    return lax.all_gather(values, "tensor", axis=0, tiled=True)


def sum_rows(values, number):
    size = lax.axis_size("tensor")
    blocks = values.astype(jnp.bfloat16).reshape(size, -1, values.shape[1])
    return jnp.sum(exchange("tensor", True, number, blocks)[0].astype(jnp.float32), axis=0)


MESH = pl.DeviceIdType.MESH
ANY = pl.BlockSpec(memory_space=pl.ANY)
VMEM = pl.BlockSpec(memory_space=pltpu.VMEM)
PAIR = 2


def greet(position, length, mate, below, above):
    barrier = pltpu.get_barrier_semaphore()
    pl.semaphore_signal(barrier, inc=1, device_id=mate, device_id_type=MESH)

    @pl.when(position > 0)
    def _():
        pl.semaphore_signal(barrier, inc=1, device_id=below, device_id_type=MESH)

    @pl.when(position < length - 1)
    def _():
        pl.semaphore_signal(barrier, inc=1, device_id=above, device_id_type=MESH)

    inner = jnp.minimum(position, 1) + jnp.minimum(length - 1 - position, 1)
    pl.semaphore_wait(barrier, 1 + inner)


def places(length):
    me = lax.axis_index("dp")
    column = lax.axis_index("tensor")
    position, side = me // PAIR, me % PAIR
    mate = (position * PAIR + 1 - side, column)
    below = (jnp.maximum(me - PAIR, 0), column)
    above = (jnp.minimum(me + PAIR, length * PAIR - 1), column)
    return position, side, mate, below, above


def gather_kernel(length, count, *refs):
    ins, outs = refs[:count], refs[count : 2 * count]
    own_sem, send_sem, recv_sem = refs[2 * count :]
    position, side, mate, below, above = places(length)
    greet(position, length, mate, below, above)

    def copy(way, item, shard, target, source=None):
        place = outs[item].at[shard * PAIR + side]
        return pltpu.make_async_remote_copy(
            src_ref=place if source is None else source,
            dst_ref=place,
            send_sem=send_sem.at[way, item, shard],
            recv_sem=recv_sem.at[way, item, shard],
            device_id=target,
            device_id_type=MESH,
        )

    def own(item):
        return pltpu.make_async_copy(
            ins[item], outs[item].at[position * PAIR + side], own_sem.at[item]
        )

    for item in range(count):
        own(item).start()
    for step in range(length):
        for item in range(count):
            source = ins[item] if step == 0 else None
            low = position - step
            high = position + step

            @pl.when(low >= 0)
            def _(item=item, low=low, source=source, step=step):
                if step > 0:
                    copy(0, item, low, above).wait_recv()

                @pl.when(position < length - 1)
                def _():
                    copy(0, item, low, above, source).start()

                copy(2, item, low, mate, source).start()

            @pl.when(high < length)
            def _(item=item, high=high, source=source, step=step):
                if step > 0:
                    copy(1, item, high, below).wait_recv()

                @pl.when(position > 0)
                def _():
                    copy(1, item, high, below, source).start()

                if step > 0:
                    copy(2, item, high, mate).start()

    for item in range(count):
        own(item).wait()
        for shard in range(length):
            place = outs[item].at[shard * PAIR + 1 - side]
            pltpu.make_async_remote_copy(
                src_ref=place,
                dst_ref=place,
                send_sem=send_sem.at[2, item, shard],
                recv_sem=recv_sem.at[2, item, shard],
                device_id=mate,
                device_id_type=MESH,
            ).wait_recv()
            copy(2, item, shard, mate).wait_send()

            @pl.when((shard <= position) & (position < length - 1))
            def _(item=item, shard=shard):
                copy(0, item, shard, above).wait_send()

            @pl.when((shard >= position) & (position > 0))
            def _(item=item, shard=shard):
                copy(1, item, shard, below).wait_send()


def gather_weights(shards):
    dp_count = lax.axis_size("dp")
    length, count = dp_count // PAIR, len(shards)
    gathered = pl.pallas_call(
        functools.partial(gather_kernel, length, count),
        out_shape=[jax.ShapeDtypeStruct((dp_count,) + s.shape, s.dtype) for s in shards],
        in_specs=[ANY] * count,
        out_specs=[ANY] * count,
        scratch_shapes=[
            pltpu.SemaphoreType.DMA((count,)),
            pltpu.SemaphoreType.DMA((3, count, length)),
            pltpu.SemaphoreType.DMA((3, count, length)),
        ],
        compiler_params=pltpu.CompilerParams(collective_id=0, has_side_effects=True),
    )(*shards)
    return [g.reshape(dp_count * g.shape[1], g.shape[2]) for g in gathered]


def scatter_kernel(length, count, *refs):
    ins, outs = refs[:count], refs[count : 2 * count]
    swap_refs = refs[2 * count : 3 * count]
    sent_refs = refs[3 * count : 4 * count]
    line_refs = refs[4 * count : 5 * count]
    send_sem, recv_sem = refs[5 * count :]
    position, side, mate, below, above = places(length)
    greet(position, length, mate, below, above)
    order = []
    for step in range(length):
        for target in (length - 1 - step, step):
            if target not in order:
                order.append(target)

    def swap(item, target):
        return pltpu.make_async_remote_copy(
            src_ref=ins[item].at[target * PAIR + 1 - side],
            dst_ref=swap_refs[item].at[target],
            send_sem=send_sem.at[2, item, target],
            recv_sem=recv_sem.at[2, item, target],
            device_id=mate,
            device_id_type=MESH,
        )

    def hop(way, item, target):
        return pltpu.make_async_remote_copy(
            src_ref=sent_refs[item].at[target],
            dst_ref=line_refs[item].at[way, target],
            send_sem=send_sem.at[way, item, target],
            recv_sem=recv_sem.at[way, item, target],
            device_id=above if way == 0 else below,
            device_id_type=MESH,
        )

    def paired(item, target):
        swap(item, target).wait_recv()
        mine = ins[item][target * PAIR + side].astype(jnp.float32)
        return mine + swap_refs[item][target].astype(jnp.float32)

    for target in order:
        for item in range(count):
            swap(item, target).start()
    for target in order:
        for item in range(count):
            for way, passes, inner in (
                (0, position < target, position > 0),
                (1, position > target, position < length - 1),
            ):

                @pl.when(passes)
                def _(way=way, inner=inner, item=item, target=target):
                    kind = sent_refs[item].dtype

                    @pl.when(inner)
                    def _():
                        hop(way, item, target).wait_recv()
                        total = paired(item, target) + line_refs[item][way, target].astype(
                            jnp.float32
                        )
                        sent_refs[item][target] = total.astype(kind)

                    @pl.when(jnp.logical_not(inner))
                    def _():
                        sent_refs[item][target] = paired(item, target).astype(kind)

                    hop(way, item, target).start()

    for item in range(count):
        for target in range(length):

            @pl.when(position == target)
            def _(item=item, target=target):
                outs[item][...] = paired(item, target)
                if target > 0:
                    hop(0, item, target).wait_recv()
                    outs[item][...] += line_refs[item][0, target].astype(jnp.float32)
                if target < length - 1:
                    hop(1, item, target).wait_recv()
                    outs[item][...] += line_refs[item][1, target].astype(jnp.float32)

            @pl.when(position < target)
            def _(item=item, target=target):
                hop(0, item, target).wait_send()

            @pl.when(position > target)
            def _(item=item, target=target):
                hop(1, item, target).wait_send()

            swap(item, target).wait_send()


def scatter_gradients(totals):
    dp_count = lax.axis_size("dp")
    length, count = dp_count // PAIR, len(totals)
    kind = jnp.bfloat16
    parts = [t.astype(kind).reshape(dp_count, t.shape[0] // dp_count, t.shape[1]) for t in totals]
    shapes = [p.shape[1:] for p in parts]
    return pl.pallas_call(
        functools.partial(scatter_kernel, length, count),
        out_shape=[jax.ShapeDtypeStruct(s, jnp.float32) for s in shapes],
        in_specs=[VMEM] * count,
        out_specs=[VMEM] * count,
        scratch_shapes=[pltpu.VMEM((length,) + s, kind) for s in shapes]
        + [pltpu.VMEM((length,) + s, kind) for s in shapes]
        + [pltpu.VMEM((2, length) + s, kind) for s in shapes]
        + [
            pltpu.SemaphoreType.DMA((3, count, length)),
            pltpu.SemaphoreType.DMA((3, count, length)),
        ],
        compiler_params=pltpu.CompilerParams(collective_id=1, has_side_effects=True),
    )(*parts)


def exchange_kernel(axis, size, spread, count, *refs):
    ins, outs = refs[:count], refs[count : 2 * count]
    own_sem, send_sem, recv_sem = refs[2 * count :]
    me = lax.axis_index(axis)
    barrier = pltpu.get_barrier_semaphore()

    def peer(shift):
        other = lax.rem(me + shift, size)
        places = {name: lax.axis_index(name) for name in ("dp", "tensor")}
        places[axis] = other
        return other, (places["dp"], places["tensor"])

    def send(item, shift):
        other, target = peer(shift)
        return pltpu.make_async_remote_copy(
            src_ref=ins[item].at[other] if spread else ins[item],
            dst_ref=outs[item].at[me],
            send_sem=send_sem.at[item, shift - 1],
            recv_sem=recv_sem.at[item, shift - 1],
            device_id=target,
            device_id_type=MESH,
        )

    def arrive(item, shift):
        other, target = peer(size - shift)
        return pltpu.make_async_remote_copy(
            src_ref=outs[item].at[other],
            dst_ref=outs[item].at[other],
            send_sem=send_sem.at[item, shift - 1],
            recv_sem=recv_sem.at[item, shift - 1],
            device_id=target,
            device_id_type=MESH,
        )

    def own(item):
        source = ins[item].at[me] if spread else ins[item]
        return pltpu.make_async_copy(source, outs[item].at[me], own_sem.at[item])

    for shift in range(1, size):
        pl.semaphore_signal(barrier, inc=1, device_id=peer(shift)[1], device_id_type=MESH)
    for item in range(count):
        own(item).start()
    pl.semaphore_wait(barrier, size - 1)
    for item in range(count):
        for shift in range(1, size):
            send(item, shift).start()
    for item in range(count):
        own(item).wait()
        for shift in range(1, size):
            arrive(item, shift).wait_recv()
            send(item, shift).wait_send()


def exchange(axis, spread, number, *values):
    size, count = lax.axis_size(axis), len(values)
    shapes = [v.shape if spread else (size,) + v.shape for v in values]
    return pl.pallas_call(
        functools.partial(exchange_kernel, axis, size, spread, count),
        out_shape=[jax.ShapeDtypeStruct(s, v.dtype) for s, v in zip(shapes, values)],
        in_specs=[VMEM] * count,
        out_specs=[VMEM] * count,
        scratch_shapes=[
            pltpu.SemaphoreType.DMA((count,)),
            pltpu.SemaphoreType.DMA((count, size - 1)),
            pltpu.SemaphoreType.DMA((count, size - 1)),
        ],
        compiler_params=pltpu.CompilerParams(collective_id=number, has_side_effects=True),
    )(*values)


def attend(query_rows, key_rows, value_rows):
    factor = query_rows.shape[-1] ** (-0.5)
    scores = (
        jnp.einsum("blhe,bmhe->bhlm", query_rows, key_rows, preferred_element_type=jnp.float32)
        * factor
    )
    row_top = jnp.max(scores, axis=-1, keepdims=True)
    log_total = row_top + jnp.log(jnp.sum(jnp.exp(scores - row_top), axis=-1, keepdims=True))
    weights = jnp.exp(scores - log_total).astype(jnp.bfloat16)
    attended = jnp.einsum(
        "bhlm,bmhe->blhe", weights, value_rows, preferred_element_type=jnp.float32
    )
    return (attended.astype(jnp.bfloat16), log_total)


def attend_back(query_rows, key_rows, value_rows, log_total, attended_grad):
    factor = query_rows.shape[-1] ** (-0.5)
    scores = (
        jnp.einsum("blhe,bmhe->bhlm", query_rows, key_rows, preferred_element_type=jnp.float32)
        * factor
    )
    probability = jnp.exp(scores - log_total)
    weights = probability.astype(jnp.bfloat16)
    value_grad = jnp.einsum(
        "bhlm,blhe->bmhe", weights, attended_grad, preferred_element_type=jnp.float32
    )
    weight_grad = jnp.einsum(
        "blhe,bmhe->bhlm", attended_grad, value_rows, preferred_element_type=jnp.float32
    )
    row_inner = jnp.sum(probability * weight_grad, axis=-1, keepdims=True)
    score_grad = (probability * (weight_grad - row_inner) * factor).astype(jnp.bfloat16)
    query_grad = jnp.einsum(
        "bhlm,bmhe->blhe", score_grad, key_rows, preferred_element_type=jnp.float32
    )
    key_grad = jnp.einsum(
        "bhlm,blhe->bmhe", score_grad, query_rows, preferred_element_type=jnp.float32
    )
    return (query_grad, key_grad, value_grad)


def body(
    tokens,
    condition,
    adaptive_weight,
    adaptive_bias,
    entry_weight,
    entry_bias,
    output_weight,
    output_bias,
    expand_weight,
    expand_bias,
    reduce_weight,
    reduce_bias,
    cotangent,
):
    tensor_index = lax.axis_index("tensor")
    tensor_count = lax.axis_size("tensor")
    row_count = tokens.shape[0]
    features = tokens.shape[1]
    seq_count = condition.shape[0]
    local_width = adaptive_bias.shape[1]
    local_hidden = expand_bias.shape[0]
    group_rows = row_count * tensor_count
    head_count = local_width // HEAD_DIM
    head_shape = (seq_count, LEN, head_count, HEAD_DIM)
    dp_index = lax.axis_index("dp")
    dp_count = lax.axis_size("dp")
    shard_rows = adaptive_weight.shape[0]
    entry_flat = entry_weight.reshape(shard_rows, 3 * local_width)
    entry_full, output_full, expand_full, reduce_full = gather_weights(
        (entry_flat, output_weight.T, expand_weight, reduce_weight.T)
    )
    condition_float = condition.astype(jnp.float32)
    condition_all = exchange("dp", False, 2, condition)[0].reshape(-1, features)
    soft_all = jax.nn.silu(condition_all.astype(jnp.float32)).astype(jnp.bfloat16)
    soft_mine = lax.dynamic_slice_in_dim(soft_all, dp_index * shard_rows, shard_rows, 1)
    adaptive_flat = adaptive_weight.reshape(shard_rows, 6 * local_width)
    modulation_partial = jnp.dot(soft_mine, adaptive_flat, preferred_element_type=jnp.float32)
    modulation_local = (
        jnp.sum(
            exchange("dp", True, 3, modulation_partial.reshape(dp_count, seq_count, -1))[0], axis=0
        ).reshape(seq_count, 6, local_width)
        + adaptive_bias[None]
    )
    modulation = (
        exchange("tensor", False, 4, modulation_local.reshape(seq_count, -1))[0]
        .reshape(tensor_count, seq_count, 6, local_width)
        .transpose(1, 2, 0, 3)
        .reshape(seq_count, 6, features)
    )
    seq_of_row = (tensor_index * row_count + jnp.arange(row_count, dtype=jnp.int32)) // LEN
    selector = (seq_of_row[:, None] == jnp.arange(seq_count, dtype=jnp.int32)[None, :]).astype(
        jnp.float32
    )
    per_row = jnp.dot(
        selector, modulation.reshape(seq_count, 6 * features), precision=HIGHEST_PRECISION
    ).reshape(row_count, 6, features)
    shift_one, scale_one, gate_one, shift_two, scale_two, gate_two = [
        per_row[:, column] for column in range(6)
    ]
    inputs = tokens.astype(jnp.float32)
    normed_one, inverse_one = norm_rows(inputs)
    attention_local = (normed_one * (1.0 + scale_one) + shift_one).astype(jnp.bfloat16)
    attention_input = gather_rows(attention_local)
    projected = jnp.dot(
        attention_input,
        entry_full,
        preferred_element_type=jnp.float32,
    ).reshape(group_rows, 3, local_width)
    query_rows = (projected[:, 0] + entry_bias[0]).astype(jnp.bfloat16).reshape(head_shape)
    key_rows = projected[:, 1].astype(jnp.bfloat16).reshape(head_shape)
    value_rows = (projected[:, 2] + entry_bias[1]).astype(jnp.bfloat16).reshape(head_shape)
    attended, log_total = attend(query_rows, key_rows, value_rows)
    attended = attended.reshape(group_rows, local_width)
    attention_branch = (
        sum_rows(contract_last(attended, output_full), 9) + output_bias
    )
    middle = inputs + gate_one * attention_branch
    normed_two, inverse_two = norm_rows(middle)
    feed_local = (normed_two * (1.0 + scale_two) + shift_two).astype(jnp.bfloat16)
    feed_input = gather_rows(feed_local)
    hidden_pre = jnp.dot(feed_input, expand_full, preferred_element_type=jnp.float32) + expand_bias
    hidden_value, hidden_slope = gelu_pair(hidden_pre)
    hidden_rows = hidden_value.astype(jnp.bfloat16)
    feed_branch = (
        sum_rows(contract_last(hidden_rows, reduce_full), 10)
        + reduce_bias
    )
    block_output = (middle + gate_two * feed_branch).astype(jnp.bfloat16)
    upstream = cotangent.astype(jnp.float32)
    feed_grad = upstream * gate_two
    feed_gathered = gather_rows(feed_grad.astype(jnp.bfloat16))
    reduce_total = contract_first(feed_gathered, hidden_rows)
    hidden_grad = jnp.dot(feed_gathered, reduce_full, preferred_element_type=jnp.float32) * hidden_slope
    hidden_round = hidden_grad.astype(jnp.bfloat16)
    expand_total = contract_first(feed_input, hidden_round)
    feed_input_grad = sum_rows(contract_last(hidden_round, expand_full), 11)
    middle_grad = upstream + norm_back(feed_input_grad * (1.0 + scale_two), normed_two, inverse_two)
    attention_grad = middle_grad * gate_one
    attention_gathered = gather_rows(attention_grad.astype(jnp.bfloat16))
    output_total = contract_first(attention_gathered, attended)
    attended_grad = (
        jnp.dot(attention_gathered, output_full, preferred_element_type=jnp.float32)
        .astype(jnp.bfloat16)
        .reshape(head_shape)
    )
    query_grad, key_grad, value_grad = attend_back(
        query_rows, key_rows, value_rows, log_total, attended_grad
    )
    query_grad = query_grad.reshape(group_rows, local_width)
    key_grad = key_grad.reshape(group_rows, local_width)
    value_grad = value_grad.reshape(group_rows, local_width)
    entry_round = (
        jnp.stack([query_grad, key_grad, value_grad], axis=1)
        .astype(jnp.bfloat16)
        .reshape(group_rows, 3 * local_width)
    )
    entry_total = contract_first(attention_input, entry_round)
    input_grad = sum_rows(contract_last(entry_round, entry_full), 12)
    tokens_gradient = middle_grad + norm_back(
        input_grad * (1.0 + scale_one), normed_one, inverse_one
    )
    row_terms = jnp.stack(
        [
            input_grad,
            input_grad * normed_one,
            middle_grad * attention_branch,
            feed_input_grad,
            feed_input_grad * normed_two,
            upstream * feed_branch,
        ],
        axis=1,
    )
    per_sequence = lax.dot_general(
        selector,
        row_terms.reshape(row_count, 6 * features),
        (((0,), (0,)), ((), ())),
        precision=HIGHEST_PRECISION,
        preferred_element_type=jnp.float32,
    ).reshape(seq_count, 6, features)
    sequence_parts = (
        per_sequence.astype(jnp.bfloat16)
        .reshape(seq_count, 6, tensor_count, local_width)
        .transpose(2, 0, 1, 3)
        .reshape(tensor_count, seq_count, 6 * local_width)
    )
    modulation_grad = jnp.sum(
        exchange("tensor", True, 5, sequence_parts)[0].astype(jnp.float32), axis=0
    )
    own_sums = jnp.concatenate(
        [
            jnp.sum(query_grad, axis=0),
            jnp.sum(value_grad, axis=0),
            jnp.sum(hidden_grad, axis=0),
            jnp.sum(attention_grad, axis=0),
            jnp.sum(feed_grad, axis=0),
        ]
    )
    modulation_all, sums_all = exchange("dp", False, 6, modulation_grad, own_sums[None])
    modulation_all = modulation_all.reshape(dp_count * seq_count, 6 * local_width)
    dp_sums = jnp.sum(sums_all, axis=(0, 1))
    bias_adaptive = jnp.sum(modulation_all, axis=0).reshape(6, local_width)
    modulation_round = modulation_all.astype(jnp.bfloat16)
    adaptive_gradient = contract_first(soft_mine, modulation_round).reshape(
        shard_rows, 6, local_width
    )
    condition_partial = contract_last(modulation_round, adaptive_flat)
    condition_moved = exchange(
        "dp", True, 7, condition_partial.reshape(dp_count, seq_count, shard_rows)
    )[0]
    own_width = 2 * local_width + local_hidden
    condition_parts, row_parts = exchange(
        "tensor",
        False,
        8,
        condition_moved.transpose(1, 0, 2).reshape(seq_count, features),
        dp_sums[None, own_width:],
    )
    condition_sum = jnp.sum(condition_parts, axis=0)
    row_sums = jnp.sum(row_parts, axis=(0, 1))
    sigmoid_value = jax.nn.sigmoid(condition_float)
    condition_gradient = (
        condition_sum * sigmoid_value * (1.0 + condition_float * (1.0 - sigmoid_value))
    )
    entry_gradient, output_gradient, expand_gradient, reduce_gradient = scatter_gradients(
        (entry_total, output_total, expand_total, reduce_total)
    )
    entry_gradient = entry_gradient.reshape(shard_rows, 3, local_width)
    output_gradient = output_gradient.T
    reduce_gradient = reduce_gradient.T
    bias_entry = dp_sums[: 2 * local_width].reshape(2, local_width)
    bias_expand = dp_sums[2 * local_width : own_width]
    output_sums = row_sums[:features]
    reduce_sums = row_sums[features:]
    return (
        block_output,
        tokens_gradient,
        condition_gradient,
        adaptive_gradient,
        bias_adaptive,
        entry_gradient,
        bias_entry,
        output_gradient,
        output_sums,
        expand_gradient,
        bias_expand,
        reduce_gradient,
        reduce_sums,
    )


def solution(mesh):
    in_specs = (
        P(("dp", "tensor"), None),
        P("dp", None),
        P("dp", None, "tensor"),
        P(None, "tensor"),
        P("dp", None, "tensor"),
        P(None, "tensor"),
        P("tensor", "dp"),
        P(),
        P("dp", "tensor"),
        P("tensor"),
        P("tensor", "dp"),
        P(),
        P(("dp", "tensor"), None),
    )
    out_specs = (
        P(("dp", "tensor"), None),
        P(("dp", "tensor"), None),
        P("dp", None),
        P("dp", None, "tensor"),
        P(None, "tensor"),
        P("dp", None, "tensor"),
        P(None, "tensor"),
        P("tensor", "dp"),
        P(),
        P("dp", "tensor"),
        P("tensor"),
        P("tensor", "dp"),
        P(),
    )
    return jax.shard_map(body, mesh=mesh, in_specs=in_specs, out_specs=out_specs, check_vma=False)
```
